32 devices in a mesh: dp: 8 (over z, x), tensor: 4 (over y, core).
Axes of the slice: x: 2, y: 2, z: 4, core: 2. Of those that a mesh axis runs over, the one named last changes fastest.
Arguments:
- tokens: bfloat16 [16384, 768], P(('dp', 'tensor')), may hold values from -6 to 6
- lengths: int32 [8, 16], P('dp'), may hold values from 0 to 2048, as said below
- perm: int32 [16384], P(('dp', 'tensor')), may hold values from 0 to 16383, as said below
- inv: int32 [16384], P(('dp', 'tensor')), may hold values from 0 to 16383, as said below
- w_query: bfloat16 [768, 768], P('dp', 'tensor'), may hold values from -0.21875 to 0.21875
- b_query: bfloat16 [12, 64], P('tensor'), may hold values from -4 to 4
- w_key: bfloat16 [768, 768], P('dp', 'tensor'), may hold values from -0.21875 to 0.21875
- w_value: bfloat16 [768, 768], P('dp', 'tensor'), may hold values from -0.21875 to 0.21875
- b_value: bfloat16 [12, 64], P('tensor'), may hold values from -0.15625 to 0.15625
- w_out: bfloat16 [768, 768], P('tensor', 'dp'), may hold values from -3.5 to 3.5
- b_out: bfloat16 [768], replicated, may hold values from -1.5 to 1.5
- gain_one: bfloat16 [768], replicated, may hold values from 0.5 to 1.5
- bias_one: bfloat16 [768], replicated, may hold values from -1.5 to 1.5
- w_up: bfloat16 [768, 3072], P('dp', 'tensor'), may hold values from -0.21875 to 0.21875
- b_up: bfloat16 [12, 256], P('tensor'), may hold values from -1.5 to 1.5
- w_down: bfloat16 [3072, 768], P('tensor', 'dp'), may hold values from -0.109375 to 0.109375
- b_down: bfloat16 [768], replicated, may hold values from -1.5 to 1.5
- gain_two: bfloat16 [768], replicated, may hold values from 0.5 to 1.5
- bias_two: bfloat16 [768], replicated, may hold values from -1.5 to 1.5
- cotangent: bfloat16 [16384, 768], P(('dp', 'tensor')), may hold values from -6 to 6
Outputs:
- layer_output: bfloat16 [16384, 768], P(('dp', 'tensor'))
- input_grad: bfloat16 [16384, 768], P(('dp', 'tensor'))
- grad_w_query: float32 [768, 768], P('dp', 'tensor')
- grad_b_query: float32 [12, 64], P('tensor', 'dp')
- grad_w_key: float32 [768, 768], P('dp', 'tensor')
- grad_w_value: float32 [768, 768], P('dp', 'tensor')
- grad_b_value: float32 [12, 64], P('tensor', 'dp')
- grad_w_out: float32 [768, 768], P('tensor', 'dp')
- grad_b_out: float32 [768], P('dp')
- grad_gain_one: float32 [768], P('dp')
- grad_bias_one: float32 [768], P('dp')
- grad_w_up: float32 [768, 3072], P('dp', 'tensor')
- grad_b_up: float32 [12, 256], P('tensor', 'dp')
- grad_w_down: float32 [3072, 768], P('tensor', 'dp')
- grad_b_down: float32 [768], P('dp')
- grad_gain_two: float32 [768], P('dp')
- grad_bias_two: float32 [768], P('dp')
The draws below stay inside these ranges and needn't reach their ends.
Inputs may be any that keep to these rules, and one draw needn't show every extreme that they name: Row g lists, in dealt order, the lengths of the sequences packed at the start of dealt block g; zeros stand only after the last of them, and the block's remaining places are padding. Nonzero lengths are 128 or more; some row holds a single sequence of 2048. A permutation of 0 to 16383. Cut both orders into blocks of 512 places, block b belonging to dp index b // 4 and tensor index b % 4: perm sends the places of a block to blocks of the same tensor index only, exactly 64 of them to each such block. inv[perm[p]] = p for every p.
All inputs are finite; a program needn't handle non-finite values.
Results may differ from the reference program's by a relative error of at most 0.019.
Values may be sent and summed in bfloat16 or wider, within the bound.
No kernel may reach another device: no remote copies, remote signals or barrier semaphores. Data moves between devices by JAX's collectives and lax.ppermute only.
A program may use at most 192 MiB of HBM per device.

```python
import jax
import jax.numpy as jnp
from jax import lax

D = 768
H = 12
HD = 64
FF = 3072
TOK_GRP = 2048
MINLEN = 128
SLOTS = 16
GROUPS = 8
TP_WAYS = 4
TOKENS = 16384


def dealing(key):
    row_count = TOK_GRP // TP_WAYS
    per_peer = row_count // GROUPS
    device_count = GROUPS * TP_WAYS
    keys_first = jax.random.split(jax.random.fold_in(key, 11), device_count)
    keys_second = jax.random.split(jax.random.fold_in(key, 12), device_count)
    tickets = jax.vmap(lambda single: jax.random.permutation(single, row_count))(keys_first).astype(jnp.int32)
    shuffles = jax.vmap(lambda single: jax.random.permutation(single, row_count))(keys_second).astype(jnp.int32)
    devices = jnp.arange(device_count, dtype=jnp.int32)
    dest_group = devices // TP_WAYS
    tensor_place = devices % TP_WAYS
    source_group = tickets % GROUPS
    sub_place = tickets // GROUPS
    source_device = source_group * TP_WAYS + tensor_place[:, None]
    local_row = shuffles[source_device, dest_group[:, None] * per_peer + sub_place]
    perm_values = (source_device * row_count + local_row).reshape(-1).astype(jnp.int32)
    inverse = jnp.zeros((device_count * row_count,), jnp.int32).at[perm_values].set(jnp.arange(device_count * row_count, dtype=jnp.int32))
    return (perm_values, inverse)


def draw_perm(key, part):
    return dealing(key)[0]


def draw_inv(key, part):
    return dealing(key)[1]


def draw_lengths(key, part):
    picks = jax.random.randint(jax.random.fold_in(key, 21), (GROUPS, SLOTS), MINLEN, TOK_GRP // 2 + 1, dtype=jnp.int32)
    cumulative = jnp.cumsum(picks, axis=1)
    kept = jnp.where(cumulative <= TOK_GRP, picks, 0)
    full_group = jax.random.randint(jax.random.fold_in(key, 22), (), 0, GROUPS, dtype=jnp.int32)
    first_slot = jnp.arange(SLOTS, dtype=jnp.int32) == 0
    single = jnp.where(first_slot, TOK_GRP, 0).astype(jnp.int32)
    chosen = jnp.arange(GROUPS, dtype=jnp.int32)[:, None] == full_group
    return jnp.where(chosen, single[None, :], kept).astype(jnp.int32)


def shard_levels(stream_key, dims, pieces, least, largest):
    level, own = 1.0, jax.random.fold_in(stream_key, 6)
    for dim, blocks in pieces:
        heights = jnp.exp(jax.random.uniform(jax.random.fold_in(own, dim), (blocks,), jnp.float32, least / len(pieces), largest / len(pieces)))
        level = level * jnp.repeat(heights, dims[dim] // blocks).reshape([-1 if axis == dim else 1 for axis in range(len(dims))])
    return level


def gaussian(rng, dims, deviation, limit, cuts=(), kind=jnp.bfloat16):
    drawn = deviation * jax.random.normal(rng, dims, jnp.float32)
    if cuts:
        drawn = drawn * shard_levels(rng, dims, cuts, -0.22, 0.18)
    return jnp.clip(drawn, -limit, limit).astype(kind)


def setup_inputs(seed: int = 0) -> dict:
    keys = jax.random.split(jax.random.key(seed), 21)
    tokens = gaussian(keys[0], (TOKENS, D), 1.0, 6.0, ((0, 32),))
    lengths = draw_lengths(jax.random.fold_in(keys[20], 71), 0)
    perm = draw_perm(jax.random.fold_in(keys[20], 71), 0)
    inv = draw_inv(jax.random.fold_in(keys[20], 71), 0)
    w_query = gaussian(keys[4], (D, D), D ** -0.5, 0.21875, ((0, 8), (1, 4)))
    b_query = gaussian(keys[5], (H, HD), 0.3, 4.0, ((0, 4),))
    w_key = gaussian(keys[6], (D, D), D ** -0.5, 0.21875, ((0, 8), (1, 4)))
    w_value = gaussian(keys[7], (D, D), D ** -0.5, 0.21875, ((0, 8), (1, 4)))
    b_value = gaussian(keys[8], (H, HD), 0.01, 0.15625, ((0, 4),))
    w_out = gaussian(keys[9], (D, D), (max(D // 256, 2)) ** -0.5, 3.5, ((0, 4), (1, 8)))
    b_out = gaussian(keys[10], (D,), 0.1, 1.5)
    gain_one = jnp.clip(1.0 + 0.1 * jax.random.normal(keys[11], (D,), jnp.float32), 0.5, 1.5).astype(jnp.bfloat16)
    bias_one = gaussian(keys[12], (D,), 0.1, 1.5)
    w_up = gaussian(keys[13], (D, FF), D ** -0.5, 0.21875, ((0, 8), (1, 4)))
    b_up = gaussian(keys[14], (H, FF // H), 0.1, 1.5, ((0, 4),))
    w_down = gaussian(keys[15], (FF, D), FF ** -0.5, 0.109375, ((0, 4), (1, 8)))
    b_down = gaussian(keys[16], (D,), 0.1, 1.5)
    gain_two = jnp.clip(1.0 + 0.1 * jax.random.normal(keys[17], (D,), jnp.float32), 0.5, 1.5).astype(jnp.bfloat16)
    bias_two = gaussian(keys[18], (D,), 0.1, 1.5)
    cotangent = gaussian(keys[19], (TOKENS, D), 1.0, 6.0, ((0, 32),))
    return {"tokens": tokens, "lengths": lengths, "perm": perm, "inv": inv, "w_query": w_query, "b_query": b_query, "w_key": w_key, "w_value": w_value, "b_value": b_value, "w_out": w_out, "b_out": b_out, "gain_one": gain_one, "bias_one": bias_one, "w_up": w_up, "b_up": b_up, "w_down": w_down, "b_down": b_down, "gain_two": gain_two, "bias_two": bias_two, "cotangent": cotangent}


EPSILON = 1e-12
HIGHEST = lax.Precision.HIGHEST
INV_ROOT_TWO = 0.7071067811865476

@jax.custom_vjp
def low(v):
    return lax.optimization_barrier(v.astype(jnp.bfloat16)).astype(jnp.float32)

@jax.custom_vjp
def low_back(v):
    return v

def low_keep(v):
    return (low(v), None)

def low_pass(kept, grad):
    return (grad,)

def back_keep(v):
    return (v, None)

def back_low(kept, grad):
    return (low(grad),)
low.defvjp(low_keep, low_pass)
low_back.defvjp(back_keep, back_low)

def product(left, right):
    return jnp.dot(left, right, precision=HIGHEST)

def norm_rows(value, gain, bias):
    centre = value - lax.optimization_barrier(jnp.mean(value, axis=-1, keepdims=True))
    spread = lax.optimization_barrier(jnp.mean(centre * centre, axis=-1, keepdims=True))
    return centre * lax.rsqrt(spread + EPSILON) * gain + bias

def gelu_exact(value):
    return 0.5 * value * (1.0 + jax.scipy.special.erf(value * INV_ROOT_TWO))

def segment_ids(seq_lengths):
    cumulative = jnp.cumsum(seq_lengths)
    places = jnp.arange(TOK_GRP, dtype=jnp.int32)
    return lax.optimization_barrier(jnp.sum((cumulative[None, :] <= places[:, None]).astype(jnp.int32), axis=1))

def group_layer(params, block_rows, segment):
    wq, bq, wk, wv, bv, wo, bo, g1, b1, w1, c1, w2, c2, g2, b2 = params
    queries = low_back(low(product(block_rows, wq) + bq.reshape(-1)))
    key_rows = low_back(low(product(block_rows, wk)))
    values = low_back(low(product(block_rows, wv) + bv.reshape(-1)))
    head_q = queries.reshape(TOK_GRP, H, HD)
    head_k = key_rows.reshape(TOK_GRP, H, HD)
    head_v = values.reshape(TOK_GRP, H, HD)
    scores = low_back(jnp.einsum('qhd,khd->hqk', head_q, head_k, precision=HIGHEST) * 0.125)
    places = jnp.arange(TOK_GRP, dtype=jnp.int32)
    allowed = (segment[:, None] == segment[None, :]) & ((segment[:, None] < SLOTS) | (places[:, None] == places[None, :]))
    scores = jnp.where(allowed[None], scores, -1e+30)
    row_max = lax.optimization_barrier(jnp.max(scores, axis=-1, keepdims=True))
    expo = jnp.exp(scores - row_max)
    probs = expo / lax.optimization_barrier(jnp.sum(expo, axis=-1, keepdims=True))
    mixed = jnp.einsum('hqk,khd->qhd', low(probs), head_v, precision=HIGHEST).reshape(TOK_GRP, D)
    context = low_back(low(mixed))
    attended = low_back(product(context, wo) + bo)
    normed_one = norm_rows(block_rows + attended, g1, b1)
    hidden_pre = low_back(product(low(normed_one), w1) + c1.reshape(-1))
    activation = low(gelu_exact(hidden_pre))
    branch = low_back(product(activation, w2) + c2)
    return norm_rows(normed_one + branch, g2, b2)

def reference(tokens, lengths, perm, inv, w_query, b_query, w_key, w_value, b_value, w_out, b_out, gain_one, bias_one, w_up, b_up, w_down, b_down, gain_two, bias_two, cotangent):
    params = tuple((w.astype(jnp.float32) for w in (w_query, b_query, w_key, w_value, b_value, w_out, b_out, gain_one, bias_one, w_up, b_up, w_down, b_down, gain_two, bias_two)))
    dealt = tokens.astype(jnp.float32)[perm]
    cot_dealt = cotangent.astype(jnp.float32)[perm]
    segments = jax.vmap(segment_ids)(lengths)
    layer = jax.checkpoint(group_layer)

    def forward(inputs, *weights):
        blocks = inputs.reshape(GROUPS, TOK_GRP, D)
        result = lax.map(lambda element: layer(weights, element[0], element[1]), (blocks, segments))
        return result.reshape(TOKENS, D)
    layer_out, pullback = jax.vjp(forward, dealt, *params)
    gradients = pullback(cot_dealt)
    output = layer_out.astype(jnp.bfloat16)[inv]
    input_grad = gradients[0].astype(jnp.bfloat16)[inv]
    return (output, input_grad, gradients[1], gradients[2], gradients[3], gradients[4], gradients[5], gradients[6], gradients[7], gradients[8], gradients[9], gradients[10], gradients[11], gradients[12], gradients[13], gradients[14], gradients[15])
```

```python
import functools

import jax
import jax.numpy as jnp
from jax import lax
from jax.experimental import pallas as pl
from jax.experimental.pallas import tpu as pltpu
from jax.sharding import PartitionSpec as P

EPSILON = 1e-12
INV_ROOT_TWO = 0.7071067811865476
INV_ROOT_TWO_PI = 0.3989422804014327
BF = jnp.bfloat16
F32 = jnp.float32
NN = (((1,), (0,)), ((), ()))
NT = (((1,), (1,)), ((), ()))
TN = (((0,), (0,)), ((), ()))
BOTH = ("dp", "tensor")


def mm(left, right, dims):
    return lax.dot_general(left, right, dims, preferred_element_type=F32)


def swap(value, bit):
    ways = lax.axis_size("tensor")
    return lax.ppermute(value, "tensor", [(i, i ^ bit) for i in range(ways)])


def gather_group(value):
    across = swap(value, 2)
    return (value, swap(value, 1), across, swap(across, 1))


def attend_kernel(q_ref, k_ref, v_ref, segq_ref, segk_ref, ctx_ref, wide_ref, lse_ref):
    query = q_ref[...]
    keys = k_ref[...]
    values = v_ref[...]
    allowed = segq_ref[...] == segk_ref[...]
    half = lax.broadcasted_iota(jnp.int32, query.shape, 1) // 64
    mixed = jnp.zeros(query.shape, F32)
    stat = jnp.zeros(query.shape, F32)
    for head in range(2):
        mine = half == head
        scores = mm(jnp.where(mine, query, jnp.zeros_like(query)), keys, NT)
        scores = jnp.where(allowed, scores, -1e30)
        top = jnp.max(scores, axis=-1, keepdims=True)
        expo = jnp.exp(scores - top)
        total = jnp.sum(expo, axis=-1, keepdims=True)
        part = mm(expo.astype(BF), values, NN) / total
        mixed = jnp.where(mine, part, mixed)
        stat = jnp.where(mine, top + jnp.log(total), stat)
    ctx_ref[...] = mixed.astype(BF)
    wide_ref[...] = mixed
    lse_ref[...] = stat


def attend(query, keys, values, seg_col, seg_row):
    rows, width = query.shape
    total = keys.shape[0]
    block = min(256, rows)
    return pl.pallas_call(
        attend_kernel,
        grid=(width // 128, rows // block),
        in_specs=[
            pl.BlockSpec((block, 128), lambda p, i: (i, p)),
            pl.BlockSpec((total, 128), lambda p, i: (0, p)),
            pl.BlockSpec((total, 128), lambda p, i: (0, p)),
            pl.BlockSpec((block, 1), lambda p, i: (i, 0)),
            pl.BlockSpec((1, total), lambda p, i: (0, 0)),
        ],
        out_specs=[pl.BlockSpec((block, 128), lambda p, i: (i, p))] * 3,
        out_shape=[
            jax.ShapeDtypeStruct((rows, width), BF),
            jax.ShapeDtypeStruct((rows, width), F32),
            jax.ShapeDtypeStruct((rows, width), F32),
        ],
        cost_estimate=pl.CostEstimate(
            flops=16 * rows * total * width,
            bytes_accessed=16 * rows * width,
            transcendentals=rows * total * width // 64,
        ),
        name="attend",
    )(query, keys, values, seg_col, seg_row)


def attend_back_kernel(
    q_ref, g_ref, k_ref, v_ref, lse_ref, inner_ref, segq_ref, segk_ref, dq_ref, dk_ref, dv_ref, acc
):
    chunk = pl.program_id(1)
    query = q_ref[...]
    grad = g_ref[...]
    keys = k_ref[...]
    values = v_ref[...]
    allowed = segk_ref[...] == segq_ref[...]
    half = lax.broadcasted_iota(jnp.int32, query.shape, 1) // 64
    half_k = lax.broadcasted_iota(jnp.int32, keys.shape, 1) // 64
    dk = jnp.zeros(keys.shape, F32)
    dv = jnp.zeros(keys.shape, F32)
    dq = jnp.zeros(acc.shape, F32)
    for head in range(2):
        mine = half == head
        q_head = jnp.where(mine, query, jnp.zeros_like(query))
        g_head = jnp.where(mine, grad, jnp.zeros_like(grad))
        k_head = jnp.where(half_k == head, keys, jnp.zeros_like(keys))
        scores = mm(keys, q_head, NT)
        probs = jnp.where(allowed, jnp.exp(scores - lse_ref[0, head : head + 1, :]), 0.0)
        grad_probs = mm(values, g_head, NT)
        grad_scores = (probs * (grad_probs - inner_ref[0, head : head + 1, :])).astype(BF)
        dv += mm(probs.astype(BF), g_head, NN)
        dk += mm(grad_scores, q_head, NN)
        dq += mm(k_head, grad_scores, TN)
    dk_ref[...] = dk.astype(BF)
    dv_ref[...] = dv.astype(BF)

    @pl.when(chunk == 0)
    def _():
        acc[...] = dq

    @pl.when(chunk > 0)
    def _():
        acc[...] += dq

    @pl.when(chunk == pl.num_programs(1) - 1)
    def _():
        dq_ref[...] = (acc[...] * 0.125).T.astype(BF)


def attend_back(query, grad, keys, values, lse, inner, seg_row_own, seg_col_all):
    rows, width = query.shape
    total = keys.shape[0]
    block = min(512, total)
    own = pl.BlockSpec((rows, 128), lambda p, c: (0, p))
    far = pl.BlockSpec((block, 128), lambda p, c: (c, p))
    stat = pl.BlockSpec((1, 2, rows), lambda p, c: (p, 0, 0))
    return pl.pallas_call(
        attend_back_kernel,
        grid=(width // 128, total // block),
        in_specs=[
            own,
            own,
            far,
            far,
            stat,
            stat,
            pl.BlockSpec((1, rows), lambda p, c: (0, 0)),
            pl.BlockSpec((block, 1), lambda p, c: (c, 0)),
        ],
        out_specs=[own, far, far],
        out_shape=[
            jax.ShapeDtypeStruct((rows, width), BF),
            jax.ShapeDtypeStruct((total, width), BF),
            jax.ShapeDtypeStruct((total, width), BF),
        ],
        scratch_shapes=[pltpu.VMEM((128, rows), F32)],
        cost_estimate=pl.CostEstimate(
            flops=40 * rows * total * width,
            bytes_accessed=16 * total * width,
            transcendentals=rows * total * width // 64,
        ),
        name="attend_back",
    )(query, grad, keys, values, lse, inner, seg_row_own, seg_col_all)


def norm_forward(value, gain, bias):
    centre = value - jnp.mean(value, axis=-1, keepdims=True)
    spread_sq = jnp.mean(centre * centre, axis=-1, keepdims=True)
    scale = lax.rsqrt(spread_sq + EPSILON)
    normal = centre * scale
    return (normal * gain + bias, normal, scale)


def norm_backward(grad, normal, scale, gain):
    scaled = grad * gain
    return scale * (
        scaled
        - jnp.mean(scaled, axis=-1, keepdims=True)
        - normal * jnp.mean(scaled * normal, axis=-1, keepdims=True)
    )


def gelu_parts(value):
    cdf = 0.5 * (1.0 + jax.scipy.special.erf(value * INV_ROOT_TWO))
    return value * cdf, cdf + value * jnp.exp(-0.5 * value * value) * INV_ROOT_TWO_PI


def local(
    tokens,
    lengths,
    perm,
    inv,
    w_query,
    b_query,
    w_key,
    w_value,
    b_value,
    w_out,
    b_out,
    gain_one,
    bias_one,
    w_up,
    b_up,
    w_down,
    b_down,
    gain_two,
    bias_two,
    cotangent,
):
    rows, width = tokens.shape
    groups = lax.axis_size("dp")
    ways = lax.axis_size("tensor")
    me = lax.axis_index("tensor")
    per_peer = rows // groups
    part = width // groups
    cols = w_query.shape[1]
    hidden_cols = w_up.shape[1]
    slots = lengths.shape[1]
    head_count = width // 64
    iota = jnp.arange(rows, dtype=jnp.int32)

    attn_shard = jnp.concatenate((w_query, w_key, w_value, w_out.T), axis=1)
    ffn_shard = jnp.concatenate((w_up, w_down.T), axis=1)
    attn_all = lax.all_gather(attn_shard, BOTH, axis=0, tiled=True)
    ffn_all = lax.all_gather(ffn_shard, BOTH, axis=0, tiled=True)

    slot = jnp.sum((inv[None, :] < inv[:, None]).astype(jnp.int32), axis=1)
    pick = (iota[:, None] == slot[None, :]).astype(BF)

    def to_dealt(value):
        packed = mm(pick, value, NN).astype(BF).reshape(groups, per_peer, width)
        return lax.all_to_all(packed, "dp", split_axis=0, concat_axis=0, tiled=True).reshape(
            rows, width
        )

    def to_given(value):
        packed = value.reshape(groups, per_peer, width)
        moved = lax.all_to_all(packed, "dp", split_axis=0, concat_axis=0, tiled=True)
        return mm(pick, moved.reshape(rows, width), TN).astype(BF)

    x_own = to_dealt(tokens)
    cot = to_dealt(cotangent)

    source = perm // rows // ways
    earlier = (source[None, :] == source[:, None]) & (iota[None, :] < iota[:, None])
    arrival = source * per_peer + jnp.sum(earlier.astype(jnp.int32), axis=1)
    cumulative = jnp.cumsum(lengths[0])
    places = me * rows + iota
    segment = jnp.sum((cumulative[None, :] <= places[:, None]).astype(jnp.int32), axis=1)
    seg_own = jnp.sum(
        jnp.where(iota[:, None] == arrival[None, :], segment[None, :], 0), axis=1
    ).astype(BF)
    message = jnp.concatenate(
        (seg_own, b_query.reshape(-1), b_value.reshape(-1), b_up.reshape(-1))
    )
    message = jnp.stack(gather_group(message.reshape(-1, 128))).reshape(ways, -1)
    seg_all = message[:, :rows].reshape(-1).astype(jnp.int32)
    seg_all = jnp.where(
        seg_all < slots, seg_all, slots + jnp.arange(ways * rows, dtype=jnp.int32)
    )
    biases = message[:, rows:][me ^ jnp.arange(ways)].astype(F32)
    bq = biases[:, :cols].reshape(-1)
    bv = biases[:, cols : 2 * cols].reshape(-1)
    bu = biases[:, 2 * cols :].reshape(-1)

    x_all = jnp.concatenate(gather_group(x_own), axis=0)

    def whole(gathered, first, size):
        piece = gathered.reshape(groups, ways, part, -1)[:, :, :, first : first + size]
        return piece.transpose(0, 2, 1, 3).reshape(width, ways * size)

    wq, wk, wv, wo_t = (whole(attn_all, i * cols, cols) for i in range(4))
    wu = whole(ffn_all, 0, hidden_cols)
    wd_t = whole(ffn_all, hidden_cols, hidden_cols)

    query = (mm(x_own, wq, NN) + bq).astype(BF) * jnp.asarray(0.125, BF)
    keys = mm(x_all, wk, NN).astype(BF)
    values = (mm(x_all, wv, NN) + bv).astype(BF)
    context, wide, lse = attend(
        query, keys, values, seg_all[:rows].reshape(rows, 1), seg_all.reshape(1, -1)
    )

    gain_first = gain_one.astype(F32)
    gain_second = gain_two.astype(F32)
    h1 = x_own.astype(F32) + mm(context, wo_t, NT) + b_out.astype(F32)
    n1, xhat1, r1 = norm_forward(h1, gain_first, bias_one.astype(F32))
    n1b = n1.astype(BF)
    act_wide, slope = gelu_parts(mm(n1b, wu, NN) + bu)
    act = act_wide.astype(BF)
    h2 = n1 + mm(act, wd_t, NT) + b_down.astype(F32)
    y, xhat2, r2 = norm_forward(h2, gain_second, bias_two.astype(F32))
    output = to_given(y.astype(BF))

    gy = cot.astype(F32)
    g_gain2 = jnp.sum(gy * xhat2, axis=0)
    g_bias2 = jnp.sum(gy, axis=0)
    dh2 = norm_backward(gy, xhat2, r2, gain_second)
    df = dh2.astype(BF)
    g_bdown = jnp.sum(df.astype(F32), axis=0)
    g_wd_t = mm(df, act, TN)
    du = (mm(df, wd_t, NN) * slope).astype(BF)
    g_bup = jnp.sum(du.astype(F32), axis=0)
    g_wu = mm(n1b, du, TN)
    dn1 = dh2 + mm(du, wu, NT)
    g_gain1 = jnp.sum(dn1 * xhat1, axis=0)
    g_bias1 = jnp.sum(dn1, axis=0)
    dh1 = norm_backward(dn1, xhat1, r1, gain_first)
    dh1b = dh1.astype(BF)
    g_bout = jnp.sum(dh1b.astype(F32), axis=0)
    g_wo_t = mm(dh1b, context, TN)
    dctx = mm(dh1b, wo_t, NN).astype(BF)

    inner = jnp.sum((dctx.astype(F32) * wide).reshape(rows, head_count, 64), axis=-1)
    inner = inner.T.reshape(head_count // 2, 2, rows)
    lse_rows = lse.reshape(rows, head_count, 64)[:, :, 0].T.reshape(head_count // 2, 2, rows)

    def cut(grad):
        return grad.astype(BF).reshape(groups, part, ways, -1).transpose(0, 2, 1, 3)

    ffn_blocks = jnp.concatenate((cut(g_wu), cut(g_wd_t)), axis=3)
    ffn_sum = lax.psum_scatter(
        ffn_blocks.reshape(groups * ways * part, -1), BOTH, scatter_dimension=0, tiled=True
    ).astype(F32)

    dq, dk, dv = attend_back(
        query, dctx, keys, values, lse_rows, inner, seg_all[:rows].reshape(1, rows),
        seg_all.reshape(-1, 1),
    )
    terms = (mm(dk, wk, NT) + mm(dv, wv, NT)).reshape(ways, rows, width)
    mine = terms[0] + dh1 + mm(dq, wq, NT)
    sent = terms.astype(BF)
    got_own = swap(sent[1], 1)
    got_far = swap(sent[3], 1)
    across = swap((terms[2] + got_far.astype(F32)).astype(BF), 2)
    dx = (mine + got_own.astype(F32) + across.astype(F32)).astype(BF)
    input_grad = to_given(dx)

    g_wq = mm(x_own, dq, TN)
    g_wk = mm(x_all, dk, TN)
    g_wv = mm(x_all, dv, TN)
    g_bq = jnp.sum(dq.astype(F32), axis=0)
    g_bv = jnp.sum(dv.astype(F32), axis=0)

    def by_owner(vector):
        cut_dp = vector.reshape(groups, 1, part)
        return jnp.broadcast_to(cut_dp, (groups, ways, part))

    def by_head(vector, lanes):
        grid = vector.reshape(ways, -1, groups, lanes).transpose(2, 0, 1, 3)
        return grid.reshape(groups, ways, -1)

    small = jnp.concatenate(
        [by_owner(v) for v in (g_bout, g_gain1, g_bias1, g_bdown, g_gain2, g_bias2)]
        + [
            by_head(g_bq, 64 // groups),
            by_head(g_bv, 64 // groups),
            by_head(g_bup, b_up.shape[1] // groups),
        ],
        axis=2,
    )
    small_size = small.shape[2]
    small = jnp.pad(small, ((0, 0), (0, 0), (0, 16 * width - small_size)))
    attn_blocks = jnp.concatenate(
        (
            jnp.concatenate((cut(g_wq), cut(g_wk), cut(g_wv), cut(g_wo_t)), axis=3),
            small.astype(BF).reshape(groups, ways, 16, width),
        ),
        axis=2,
    )
    attn_sum = lax.psum_scatter(
        attn_blocks.reshape(groups * ways * (part + 16), width),
        BOTH,
        scatter_dimension=0,
        tiled=True,
    ).astype(F32)
    small_sum = attn_sum[part:].reshape(-1)[:small_size]
    vectors = small_sum[: 6 * part].reshape(6, part)
    rest = small_sum[6 * part :]
    heads_here = b_query.shape[0]
    per_q = heads_here * (64 // groups)
    out_bq = rest[:per_q].reshape(heads_here, -1)
    out_bv = rest[per_q : 2 * per_q].reshape(heads_here, -1)
    out_bu = rest[2 * per_q :].reshape(heads_here, -1)
    return (
        output,
        input_grad,
        attn_sum[:part, :cols],
        out_bq,
        attn_sum[:part, cols : 2 * cols],
        attn_sum[:part, 2 * cols : 3 * cols],
        out_bv,
        attn_sum[:part, 3 * cols :].T,
        vectors[0],
        vectors[1],
        vectors[2],
        ffn_sum[:, :hidden_cols],
        out_bu,
        ffn_sum[:, hidden_cols:].T,
        vectors[3],
        vectors[4],
        vectors[5],
    )


def solution(mesh):
    rows = P(BOTH, None)
    return jax.shard_map(
        local,
        mesh=mesh,
        in_specs=(
            rows,
            P("dp", None),
            P(BOTH),
            P(BOTH),
            P("dp", "tensor"),
            P("tensor", None),
            P("dp", "tensor"),
            P("dp", "tensor"),
            P("tensor", None),
            P("tensor", "dp"),
            P(),
            P(),
            P(),
            P("dp", "tensor"),
            P("tensor", None),
            P("tensor", "dp"),
            P(),
            P(),
            P(),
            rows,
        ),
        out_specs=(
            rows,
            rows,
            P("dp", "tensor"),
            P("tensor", "dp"),
            P("dp", "tensor"),
            P("dp", "tensor"),
            P("tensor", "dp"),
            P("tensor", "dp"),
            P("dp"),
            P("dp"),
            P("dp"),
            P("dp", "tensor"),
            P("tensor", "dp"),
            P("tensor", "dp"),
            P("dp"),
            P("dp"),
            P("dp"),
        ),
        check_vma=False,
    )
```

```python
import functools

import jax
import jax.numpy as jnp
from jax import lax
from jax.experimental import pallas as pl
from jax.experimental.pallas import tpu as pltpu
from jax.sharding import PartitionSpec as P

EPSILON = 1e-12
INV_ROOT_TWO = 0.7071067811865476
INV_ROOT_TWO_PI = 0.3989422804014327
BF = jnp.bfloat16
F32 = jnp.float32
NN = (((1,), (0,)), ((), ()))
NT = (((1,), (1,)), ((), ()))
TN = (((0,), (0,)), ((), ()))
BOTH = ("dp", "tensor")
SPARE = 64
BIG = 67043328


def mm(left, right, dims):
    return lax.dot_general(left, right, dims, preferred_element_type=F32)


def swap(value, bit):
    ways = lax.axis_size("tensor")
    return lax.ppermute(value, "tensor", [(i, i ^ bit) for i in range(ways)])


def gather_group(value):
    across = swap(value, 2)
    return (value, swap(value, 1), across, swap(across, 1))


def vmem(size=None):
    return pltpu.CompilerParams(vmem_limit_bytes=BIG)


def whole_spec(array):
    return pl.BlockSpec(array.shape, lambda *_: (0,) * array.ndim)


def project_kernel(x_ref, g_ref, b_ref, w_ref, q_ref, k_ref, v_ref):
    width = x_ref.shape[1]
    ways = g_ref.shape[1]
    cols = width // ways
    for t in range(ways):
        for i, base in enumerate((2 * width, 0, width)):
            piece = g_ref[:, t, :, i * cols : (i + 1) * cols].reshape(width, cols)
            w_ref[:, base + t * cols : base + (t + 1) * cols] = piece
    rows = x_ref[...]
    query = (mm(rows, w_ref[:, 2 * width :], NN) + b_ref[0:1, :]).astype(BF)
    q_ref[...] = (query.astype(F32) * 0.125).astype(BF)
    k_ref[...] = mm(rows, w_ref[:, :width], NN).astype(BF)
    v_ref[...] = (mm(rows, w_ref[:, width : 2 * width], NN) + b_ref[1:2, :]).astype(BF)


def project(x_own, gathered, bias, total):
    rows, width = x_own.shape
    own = pl.BlockSpec((rows, width), lambda i: (0, 0))
    return pl.pallas_call(
        project_kernel,
        grid=(1,),
        in_specs=[own, whole_spec(gathered), whole_spec(bias)],
        out_specs=[pl.BlockSpec((width, 3 * width), lambda i: (0, 0)), own, own, own],
        out_shape=[
            jax.ShapeDtypeStruct((width, 3 * width), BF),
            jax.ShapeDtypeStruct((rows, width), BF),
            jax.ShapeDtypeStruct((total, width), BF),
            jax.ShapeDtypeStruct((total, width), BF),
        ],
        compiler_params=vmem(),
        cost_estimate=pl.CostEstimate(
            flops=6 * rows * width * width, bytes_accessed=16 * width * width, transcendentals=0
        ),
        name="project",
    )(x_own, gathered, bias)


def project_more_kernel(x_ref, w_ref, b_ref, kin_ref, vin_ref, k_ref, v_ref):
    width = x_ref.shape[1]
    rows = x_ref[...]
    k_ref[...] = mm(rows, w_ref[:, :width], NN).astype(BF)
    v_ref[...] = (mm(rows, w_ref[:, width:], NN) + b_ref[1:2, :]).astype(BF)


def project_more(x_chunk, weights, bias, keys, values, chunk):
    rows, width = x_chunk.shape
    place = pl.BlockSpec((rows, width), lambda i: (chunk, 0))
    anywhere = pl.BlockSpec(memory_space=pl.ANY)
    return pl.pallas_call(
        project_more_kernel,
        grid=(1,),
        in_specs=[
            whole_spec(x_chunk),
            pl.BlockSpec((width, 2 * width), lambda i: (0, 0)),
            whole_spec(bias),
            anywhere,
            anywhere,
        ],
        out_specs=[place, place],
        out_shape=[jax.ShapeDtypeStruct(keys.shape, BF)] * 2,
        input_output_aliases={3: 0, 4: 1},
        compiler_params=vmem(),
        cost_estimate=pl.CostEstimate(
            flops=4 * rows * width * width, bytes_accessed=8 * width * width, transcendentals=0
        ),
        name="project_more",
    )(x_chunk, weights, bias, keys, values)


def attend_kernel(q_ref, k_ref, v_ref, segq_ref, segk_ref, ctx_ref, wide_ref, lse_ref):
    query = q_ref[...]
    keys = k_ref[...]
    values = v_ref[...]
    allowed = segq_ref[...] == segk_ref[...]
    half = lax.broadcasted_iota(jnp.int32, query.shape, 1) // 64
    mixed = jnp.zeros(query.shape, F32)
    stat = jnp.zeros(query.shape, F32)
    for head in range(2):
        mine = half == head
        scores = mm(jnp.where(mine, query, jnp.zeros_like(query)), keys, NT)
        scores = jnp.where(allowed, scores, -1e30)
        top = jnp.max(scores, axis=-1, keepdims=True)
        expo = jnp.exp(scores - top)
        total = jnp.sum(expo, axis=-1, keepdims=True)
        part = mm(expo.astype(BF), values, NN) / total
        mixed = jnp.where(mine, part, mixed)
        stat = jnp.where(mine, top + jnp.log(total), stat)
    ctx_ref[...] = mixed.astype(BF)
    wide_ref[...] = mixed
    turned = stat.T
    lse_ref[0, 0:1, :] = turned[0:1, :]
    lse_ref[0, 1:2, :] = turned[64:65, :]


def attend(query, keys, values, seg_col, seg_row):
    rows, width = query.shape
    total = keys.shape[0]
    block = min(256, rows)
    pairs = width // 128
    mine = pl.BlockSpec((block, 128), lambda p, i: (i, p))
    return pl.pallas_call(
        attend_kernel,
        grid=(pairs, rows // block),
        in_specs=[
            mine,
            pl.BlockSpec((total, 128), lambda p, i: (0, p)),
            pl.BlockSpec((total, 128), lambda p, i: (0, p)),
            pl.BlockSpec((block, 1), lambda p, i: (i, 0)),
            pl.BlockSpec((1, total), lambda p, i: (0, 0)),
        ],
        out_specs=[mine, mine, pl.BlockSpec((1, 2, block), lambda p, i: (p, 0, i))],
        out_shape=[
            jax.ShapeDtypeStruct((rows, width), BF),
            jax.ShapeDtypeStruct((rows, width), F32),
            jax.ShapeDtypeStruct((pairs, 2, rows), F32),
        ],
        compiler_params=vmem(),
        cost_estimate=pl.CostEstimate(
            flops=16 * rows * total * width,
            bytes_accessed=16 * rows * width,
            transcendentals=rows * total * width // 64,
        ),
        name="attend",
    )(query, keys, values, seg_col, seg_row)


def attend_back_kernel(last, *refs):
    q_ref, g_ref, k_ref, v_ref, lse_ref, inner_ref, segq_ref, segk_ref = refs[:8]
    before_ref = refs[8] if last else None
    dq_ref, dk_ref, dv_ref, acc = refs[-4:]
    chunk = pl.program_id(1)
    query = q_ref[...]
    grad = g_ref[...]
    keys = k_ref[...]
    values = v_ref[...]
    allowed = segk_ref[...] == segq_ref[...]
    half = lax.broadcasted_iota(jnp.int32, query.shape, 1) // 64
    half_k = lax.broadcasted_iota(jnp.int32, keys.shape, 1) // 64
    dk = jnp.zeros(keys.shape, F32)
    dv = jnp.zeros(keys.shape, F32)
    dq = jnp.zeros(acc.shape, F32)
    for head in range(2):
        mine = half == head
        q_head = jnp.where(mine, query, jnp.zeros_like(query))
        g_head = jnp.where(mine, grad, jnp.zeros_like(grad))
        k_head = jnp.where(half_k == head, keys, jnp.zeros_like(keys))
        scores = mm(keys, q_head, NT)
        probs = jnp.where(allowed, jnp.exp(scores - lse_ref[0, head : head + 1, :]), 0.0)
        grad_probs = mm(values, g_head, NT)
        grad_scores = (probs * (grad_probs - inner_ref[0, head : head + 1, :])).astype(BF)
        dv += mm(probs.astype(BF), g_head, NN)
        dk += mm(grad_scores, q_head, NN)
        dq += mm(k_head, grad_scores, TN)
    dk_ref[...] = dk.astype(BF)
    dv_ref[...] = dv.astype(BF)

    @pl.when(chunk == 0)
    def _():
        acc[...] = before_ref[...] + dq if last else dq

    @pl.when(chunk > 0)
    def _():
        acc[...] += dq

    @pl.when(chunk == pl.num_programs(1) - 1)
    def _():
        dq_ref[...] = (acc[...] * 0.125).T.astype(BF) if last else acc[...]


def attend_back(query, grad, keys, values, lse, inner, seg_row, seg_col, base, before):
    rows, width = query.shape
    last = before is not None
    own = pl.BlockSpec((rows, 128), lambda p, c: (0, p))
    far = pl.BlockSpec((rows, 128), lambda p, c: (base - c, p))
    out = pl.BlockSpec((rows, 128), lambda p, c: (c, p))
    stat = pl.BlockSpec((1, 2, rows), lambda p, c: (p, 0, 0))
    turned = pl.BlockSpec((128, rows), lambda p, c: (p, 0))
    if last:
        dq_spec, dq_shape = own, jax.ShapeDtypeStruct((rows, width), BF)
    else:
        dq_spec, dq_shape = turned, jax.ShapeDtypeStruct((width, rows), F32)
    return pl.pallas_call(
        functools.partial(attend_back_kernel, last),
        grid=(width // 128, 2),
        in_specs=[
            own,
            own,
            far,
            far,
            stat,
            stat,
            pl.BlockSpec((1, rows), lambda p, c: (0, 0)),
            pl.BlockSpec((rows, 1), lambda p, c: (base - c, 0)),
        ]
        + ([turned] if last else []),
        out_specs=[dq_spec, out, out],
        out_shape=[
            dq_shape,
            jax.ShapeDtypeStruct((2 * rows, width), BF),
            jax.ShapeDtypeStruct((2 * rows, width), BF),
        ],
        scratch_shapes=[pltpu.VMEM((128, rows), F32)],
        compiler_params=vmem(),
        cost_estimate=pl.CostEstimate(
            flops=80 * rows * rows * width,
            bytes_accessed=32 * rows * width,
            transcendentals=rows * rows * width // 32,
        ),
        name="attend_back",
    )(query, grad, keys, values, lse, inner, seg_row, seg_col, *([before] if last else []))


def tile_rows(vectors, count):
    row = lax.broadcasted_iota(jnp.int32, (count, SPARE), 0)
    tile = jnp.zeros((count, SPARE), F32)
    at = 0
    for vector in vectors:
        for first in range(0, vector.shape[1], SPARE):
            tile = jnp.where(row == at, vector[:, first : first + SPARE], tile)
            at += 1
    return tile


def middle_kernel(
    x_ref, ctx_ref, wide_ref, cot_ref, vec_ref, bu_ref, wu_ref, wd_ref, tail_ref,
    y_ref, dh1_ref, dctx_ref, inner_ref, small_ref, grads_ref,
    wo, xhat, scale, n1b, acc, act, slope, df, gmain, gtail, sems,
):
    step = pl.program_id(0)
    ways = tail_ref.shape[1]
    outer, inner_rows = tail_ref.shape[0], tail_ref.shape[2]
    rows, width = x_ref.shape
    cols = width // ways

    def vec(i):
        return vec_ref[i : i + 1, :]

    @pl.when(step == 0)
    def _():
        for t in range(ways):
            wo[:, t * cols : (t + 1) * cols] = tail_ref[:, t, :, :cols].reshape(width, cols)
        h1 = x_ref[...].astype(F32) + mm(ctx_ref[...], wo[...], NT) + vec(0)
        n1, normal, size = norm_forward(h1, vec(1), vec(2))
        xhat[...] = normal
        scale[...] = size
        n1b[...] = n1.astype(BF)
        acc[...] = n1 + vec(3)

    @pl.when(step < ways)
    def _():
        pre = mm(n1b[...], wu_ref[...].reshape(width, width), NN) + bu_ref[0]
        value, rate = gelu_parts(pre)
        value = value.astype(BF)
        act[step] = value
        slope[step] = rate
        acc[...] += mm(value, wd_ref[...].reshape(width, width), NT)

    @pl.when(step == ways - 1)
    def _():
        y, normal, size = norm_forward(acc[...], vec(4), vec(5))
        y_ref[...] = y.astype(BF)
        grad = cot_ref[...].astype(F32)
        small_ref[4:5, :] = jnp.sum(grad * normal, axis=0, keepdims=True)
        small_ref[5:6, :] = jnp.sum(grad, axis=0, keepdims=True)
        dh2 = norm_backward(grad, normal, size, vec(4))
        low = dh2.astype(BF)
        df[...] = low
        small_ref[3:4, :] = jnp.sum(low.astype(F32), axis=0, keepdims=True)
        acc[...] = dh2

    def main_copy(t):
        return pltpu.make_async_copy(
            gmain.at[t], grads_ref.at[:, t, :, pl.ds(0, 2 * width)], sems.at[t]
        )

    def tail_copy(t):
        return pltpu.make_async_copy(
            gtail.at[t], grads_ref.at[:, t, :, pl.ds(2 * width, cols + SPARE)], sems.at[ways + t]
        )

    @pl.when(step >= ways)
    def _():
        t = step - ways
        du = (mm(df[...], wd_ref[...].reshape(width, width), NN) * slope[t]).astype(BF)
        small_ref[pl.ds(8 + t, 1), :] = jnp.sum(du.astype(F32), axis=0, keepdims=True)
        shape = (outer, inner_rows, width)
        gmain[t, :, :, :width] = mm(n1b[...], du, TN).astype(BF).reshape(shape)
        gmain[t, :, :, width:] = mm(df[...], act[t], TN).astype(BF).reshape(shape)
        main_copy(t).start()
        acc[...] += mm(du, wu_ref[...].reshape(width, width), NT)

    @pl.when(step == 2 * ways - 1)
    def _():
        dn1 = acc[...]
        normal = xhat[...]
        small_ref[1:2, :] = jnp.sum(dn1 * normal, axis=0, keepdims=True)
        small_ref[2:3, :] = jnp.sum(dn1, axis=0, keepdims=True)
        dh1 = norm_backward(dn1, normal, scale[...], vec(1))
        low = dh1.astype(BF)
        dh1_ref[...] = dh1
        small_ref[0:1, :] = jnp.sum(low.astype(F32), axis=0, keepdims=True)
        g_wo = mm(low, ctx_ref[...], TN).astype(BF)
        spare = jnp.zeros((width // outer, SPARE), F32)
        vectors = [small_ref[i : i + 1, :] for i in range(6)]
        for t in range(ways):
            gtail[t, :, :, :cols] = g_wo[:, t * cols : (t + 1) * cols].reshape(
                outer, inner_rows, cols
            )
            if outer > 1:
                spare = tile_rows([small_ref[8 + t : 9 + t, :]] + vectors, inner_rows)
                for g in range(outer):
                    gtail[t, g, :, cols:] = spare.astype(BF)
            else:
                gtail[t, :, :, cols:] = jnp.zeros((outer, inner_rows, SPARE), BF)
            tail_copy(t).start()
        dctx = mm(low, wo[...], NN).astype(BF)
        dctx_ref[...] = dctx
        head = lax.broadcasted_iota(jnp.int32, (16, width), 0)
        lane = lax.broadcasted_iota(jnp.int32, (16, width), 1) // 64
        inner_ref[...] = lax.dot_general(
            (head == lane).astype(F32),
            dctx.astype(F32) * wide_ref[...],
            NT,
            preferred_element_type=F32,
            precision=lax.Precision.HIGHEST,
        )
        for t in range(ways):
            main_copy(t).wait()
            tail_copy(t).wait()


def middle(x_own, context, wide, cot, vectors, bu, gathered):
    rows, width = x_own.shape
    outer, ways, inner_rows, lanes = gathered.shape
    cols = width // ways
    half = (outer, 1, inner_rows, width)
    return pl.pallas_call(
        middle_kernel,
        grid=(2 * ways,),
        in_specs=[
            whole_spec(x_own),
            whole_spec(context),
            whole_spec(wide),
            whole_spec(cot),
            whole_spec(vectors),
            pl.BlockSpec((1, 1, width), lambda s: (lax.rem(s, ways), 0, 0)),
            pl.BlockSpec(half, lambda s: (0, lax.rem(s, ways), 0, 0)),
            pl.BlockSpec(half, lambda s: (0, lax.rem(s, ways), 0, 1)),
            pl.BlockSpec(
                (outer, ways, inner_rows, cols + SPARE),
                lambda s: (0, 0, 0, 2 * width // (cols + SPARE)),
            ),
        ],
        out_specs=[
            whole_spec(x_own),
            whole_spec(x_own),
            whole_spec(x_own),
            pl.BlockSpec((16, rows), lambda s: (0, 0)),
            pl.BlockSpec((16, width), lambda s: (0, 0)),
            pl.BlockSpec(memory_space=pl.ANY),
        ],
        out_shape=[
            jax.ShapeDtypeStruct((rows, width), BF),
            jax.ShapeDtypeStruct((rows, width), F32),
            jax.ShapeDtypeStruct((rows, width), BF),
            jax.ShapeDtypeStruct((16, rows), F32),
            jax.ShapeDtypeStruct((16, width), F32),
            jax.ShapeDtypeStruct(gathered.shape, BF),
        ],
        scratch_shapes=[
            pltpu.VMEM((width, width), BF),
            pltpu.VMEM((rows, width), F32),
            pltpu.VMEM((rows, 1), F32),
            pltpu.VMEM((rows, width), BF),
            pltpu.VMEM((rows, width), F32),
            pltpu.VMEM((ways, rows, width), BF),
            pltpu.VMEM((ways, rows, width), F32),
            pltpu.VMEM((rows, width), BF),
            pltpu.VMEM((ways, outer, inner_rows, 2 * width), BF),
            pltpu.VMEM((ways, outer, inner_rows, cols + SPARE), BF),
            pltpu.SemaphoreType.DMA((2 * ways,)),
        ],
        compiler_params=vmem(),
        cost_estimate=pl.CostEstimate(
            flops=54 * rows * width * width,
            bytes_accessed=64 * width * width,
            transcendentals=8 * rows * width,
        ),
        name="middle",
    )(x_own, context, wide, cot, vectors, bu, gathered, gathered, gathered)


def terms_kernel(last, *refs):
    dk_ref, dv_ref, w_ref = refs[:3]
    first_ref, second_ref = refs[-2:]
    rows, width = first_ref.shape
    for i, out_ref in enumerate((first_ref, second_ref)):
        value = mm(dk_ref[i * rows : (i + 1) * rows, :], w_ref[:, :width], NT)
        value += mm(dv_ref[i * rows : (i + 1) * rows, :], w_ref[:, width : 2 * width], NT)
        if last and i == 1:
            value += mm(refs[3][...], w_ref[:, 2 * width :], NT) + refs[4][...]
        out_ref[...] = value.astype(out_ref.dtype)


def terms(dk, dv, weights, dq=None, dh1=None):
    rows, width = dk.shape[0] // 2, dk.shape[1]
    last = dq is not None
    args = (dk, dv, weights) + ((dq, dh1) if last else ())
    out = pl.BlockSpec((rows, width), lambda i: (0, 0))
    in_specs = [whole_spec(a) for a in args]
    if not last:
        in_specs[2] = pl.BlockSpec((width, 2 * width), lambda i: (0, 0))
    return pl.pallas_call(
        functools.partial(terms_kernel, last),
        grid=(1,),
        in_specs=in_specs,
        out_specs=[out, out],
        out_shape=[
            jax.ShapeDtypeStruct((rows, width), BF),
            jax.ShapeDtypeStruct((rows, width), F32),
        ],
        compiler_params=vmem(),
        cost_estimate=pl.CostEstimate(
            flops=8 * rows * width * width, bytes_accessed=8 * width * width, transcendentals=0
        ),
        name="terms",
    )(*args)


def weight_grads_kernel(x0, x1, x2, x3, dka, dva, dkb, dvb, dq_ref, out_ref, small_ref):
    rows, width = x0.shape
    outer, ways, inner_rows, _ = out_ref.shape
    cols = width // ways

    def keep(grad, i):
        low = grad.astype(BF)
        for t in range(ways):
            out_ref[:, t, :, i * cols : (i + 1) * cols] = low[:, t * cols : (t + 1) * cols].reshape(
                outer, inner_rows, cols
            )

    def over_chunks(high, low):
        return (
            mm(x3[...], high[:rows, :], TN)
            + mm(x2[...], high[rows:, :], TN)
            + mm(x1[...], low[:rows, :], TN)
            + mm(x0[...], low[rows:, :], TN)
        )

    keep(mm(x0[...], dq_ref[...], TN), 0)
    keep(over_chunks(dka, dkb), 1)
    keep(over_chunks(dva, dvb), 2)
    g_bq = jnp.sum(dq_ref[...].astype(F32), axis=0, keepdims=True)
    g_bv = jnp.sum(dva[...].astype(F32), axis=0, keepdims=True)
    g_bv += jnp.sum(dvb[...].astype(F32), axis=0, keepdims=True)
    small_ref[0:1, :] = g_bq
    small_ref[1:2, :] = g_bv
    for t in range(ways):
        if outer > 1:
            here = slice(t * cols, (t + 1) * cols)
            spare = tile_rows([g_bq[:, here], g_bv[:, here]], inner_rows).astype(BF)
            for g in range(outer):
                out_ref[g, t, :, 3 * cols :] = spare
        else:
            out_ref[:, t, :, 3 * cols :] = jnp.zeros((outer, inner_rows, SPARE), BF)


def weight_grads(chunks, dka, dva, dkb, dvb, dq, shape):
    width = dq.shape[1]
    rows = dq.shape[0]
    args = (*chunks, dka, dva, dkb, dvb, dq)
    return pl.pallas_call(
        weight_grads_kernel,
        grid=(1,),
        in_specs=[whole_spec(a) for a in args],
        out_specs=[
            pl.BlockSpec(shape, lambda i: (0, 0, 0, 0)),
            pl.BlockSpec((8, width), lambda i: (0, 0)),
        ],
        out_shape=[jax.ShapeDtypeStruct(shape, BF), jax.ShapeDtypeStruct((8, width), F32)],
        compiler_params=vmem(),
        cost_estimate=pl.CostEstimate(
            flops=18 * rows * width * width, bytes_accessed=16 * width * width, transcendentals=0
        ),
        name="weight_grads",
    )(*args)


def norm_forward(value, gain, bias):
    centre = value - jnp.mean(value, axis=-1, keepdims=True)
    spread_sq = jnp.mean(centre * centre, axis=-1, keepdims=True)
    scale = lax.rsqrt(spread_sq + EPSILON)
    normal = centre * scale
    return (normal * gain + bias, normal, scale)


def norm_backward(grad, normal, scale, gain):
    scaled = grad * gain
    return scale * (
        scaled
        - jnp.mean(scaled, axis=-1, keepdims=True)
        - normal * jnp.mean(scaled * normal, axis=-1, keepdims=True)
    )


def gelu_parts(value):
    cdf = 0.5 * (1.0 + jax.scipy.special.erf(value * INV_ROOT_TWO))
    return value * cdf, cdf + value * jnp.exp(-0.5 * value * value) * INV_ROOT_TWO_PI


def local(
    tokens,
    lengths,
    perm,
    inv,
    w_query,
    b_query,
    w_key,
    w_value,
    b_value,
    w_out,
    b_out,
    gain_one,
    bias_one,
    w_up,
    b_up,
    w_down,
    b_down,
    gain_two,
    bias_two,
    cotangent,
):
    rows, width = tokens.shape
    groups = lax.axis_size("dp")
    ways = lax.axis_size("tensor")
    me_dp = lax.axis_index("dp")
    me = lax.axis_index("tensor")
    per_peer = rows // groups
    part = width // groups
    cols = w_query.shape[1]
    slots = lengths.shape[1]
    heads_here = b_query.shape[0]
    aligned = part % 16 == 0 and part >= 96
    outer, inner_rows = (groups, part) if aligned else (1, width)
    iota = jnp.arange(rows, dtype=jnp.int32)

    def for_kernel(gathered):
        grid = gathered.reshape(groups, ways, part, -1)
        if aligned:
            return grid
        return grid.transpose(1, 0, 2, 3).reshape(1, ways, width, -1)

    def for_owners(grads):
        if not aligned:
            grads = grads.reshape(ways, groups, part, -1).transpose(1, 0, 2, 3)
        return grads.reshape(groups * ways * part, -1)

    def gather_shards(shard):
        return for_kernel(lax.all_gather(shard, BOTH, axis=0, tiled=True))

    def sum_shards(grads):
        return lax.psum_scatter(
            for_owners(grads), BOTH, scatter_dimension=0, tiled=True
        ).astype(F32)

    spare = jnp.zeros((part, SPARE), BF)
    qkv_shard = jnp.concatenate((w_query, w_key, w_value, spare), axis=1)
    ffn_shard = jnp.concatenate((w_up, w_down.T, w_out.T, spare), axis=1)
    qkv_all = gather_shards(qkv_shard)
    ffn_all = gather_shards(ffn_shard)

    slot = jnp.sum((inv[None, :] < inv[:, None]).astype(jnp.int32), axis=1)
    pick = (iota[:, None] == slot[None, :]).astype(BF)

    def to_dealt(value):
        packed = mm(pick, value, NN).astype(BF).reshape(groups, per_peer, width)
        return lax.all_to_all(packed, "dp", split_axis=0, concat_axis=0, tiled=True).reshape(
            rows, width
        )

    def to_given(value):
        packed = value.reshape(groups, per_peer, width)
        moved = lax.all_to_all(packed, "dp", split_axis=0, concat_axis=0, tiled=True)
        return mm(pick, moved.reshape(rows, width), TN).astype(BF)

    x_own = to_dealt(tokens)
    cot = to_dealt(cotangent)

    source = perm // rows // ways
    earlier = (source[None, :] == source[:, None]) & (iota[None, :] < iota[:, None])
    arrival = source * per_peer + jnp.sum(earlier.astype(jnp.int32), axis=1)
    cumulative = jnp.cumsum(lengths[0])
    places = me * rows + iota
    segment = jnp.sum((cumulative[None, :] <= places[:, None]).astype(jnp.int32), axis=1)
    seg_own = jnp.sum(
        jnp.where(iota[:, None] == arrival[None, :], segment[None, :], 0), axis=1
    ).astype(BF)
    message = jnp.concatenate(
        (seg_own, b_query.reshape(-1), b_value.reshape(-1), b_up.reshape(-1))
    )
    message = jnp.stack(gather_group(message.reshape(-1, 128))).reshape(ways, -1)
    seg_all = message[:, :rows].reshape(-1).astype(jnp.int32)
    seg_all = jnp.where(
        seg_all < slots, seg_all, slots + jnp.arange(ways * rows, dtype=jnp.int32)
    )
    biases = message[:, rows:][me ^ jnp.arange(ways)].astype(F32)
    qv_bias = jnp.stack(
        (biases[:, :cols].reshape(-1), biases[:, cols : 2 * cols].reshape(-1))
    )
    up_bias = biases[:, 2 * cols :].reshape(ways, 1, -1)
    vectors = jnp.stack(
        (b_out, gain_one, bias_one, b_down, gain_two, bias_two, b_out, b_out)
    ).astype(F32)

    chunks = gather_group(x_own)
    weights, query, keys, values = project(x_own, qkv_all, qv_bias, ways * rows)
    for i in range(1, ways):
        keys, values = project_more(chunks[i], weights, qv_bias, keys, values, i)
    context, wide, lse = attend(
        query, keys, values, seg_all[:rows].reshape(rows, 1), seg_all.reshape(1, -1)
    )
    y, dh1, dctx, inner, small_ffn, ffn_grads = middle(
        x_own, context, wide, cot, vectors, up_bias, ffn_all
    )
    output = to_given(y)
    ffn_sum = sum_shards(ffn_grads)

    inner = inner[: width // 64].reshape(lse.shape)
    seg_row = seg_all[:rows].reshape(1, rows)
    seg_col = seg_all.reshape(-1, 1)
    dq_part, dka, dva = attend_back(
        query, dctx, keys, values, lse, inner, seg_row, seg_col, 3, None
    )
    term_3, term_2 = terms(dka, dva, weights)
    far = (term_2 + swap(term_3, 1).astype(F32)).astype(BF)
    across = swap(far, 2)
    dq, dkb, dvb = attend_back(
        query, dctx, keys, values, lse, inner, seg_row, seg_col, 1, dq_part
    )
    qkv_grads, small_qkv = weight_grads(chunks, dka, dva, dkb, dvb, dq, qkv_all.shape)
    term_1, mine = terms(dkb, dvb, weights, dq, dh1)
    near = swap(term_1, 1)
    input_grad = to_given((mine + near.astype(F32) + across.astype(F32)).astype(BF))
    qkv_sum = sum_shards(qkv_grads)

    def my_lanes(vector, count):
        lanes = vector.reshape(heads_here, groups, -1)
        return lax.dynamic_index_in_dim(lanes, me_dp, 1, keepdims=False)

    if aligned:
        from_ffn = ffn_sum[:, 2 * width + cols :].reshape(-1)
        g_bup = from_ffn[:width]
        by_width = from_ffn[width : 7 * width].reshape(6, width)
        from_qkv = qkv_sum[:, 3 * cols :].reshape(-1)
        g_bq, g_bv = from_qkv[:cols], from_qkv[cols : 2 * cols]
    else:
        small = lax.psum(jnp.concatenate((small_ffn, small_qkv)).astype(BF), BOTH).astype(F32)
        by_width = small[:6]
        g_bup = lax.dynamic_index_in_dim(small, 8 + me, 0, keepdims=False)
        g_bq = lax.dynamic_slice_in_dim(small[16], me * cols, cols)
        g_bv = lax.dynamic_slice_in_dim(small[17], me * cols, cols)
    by_owner = lax.dynamic_slice_in_dim(by_width, me_dp * part, part, 1)
    return (
        output,
        input_grad,
        qkv_sum[:, :cols],
        my_lanes(g_bq, 0),
        qkv_sum[:, cols : 2 * cols],
        qkv_sum[:, 2 * cols : 3 * cols],
        my_lanes(g_bv, 0),
        ffn_sum[:, 2 * width : 2 * width + cols].T,
        by_owner[0],
        by_owner[1],
        by_owner[2],
        ffn_sum[:, :width],
        my_lanes(g_bup, 0),
        ffn_sum[:, width : 2 * width].T,
        by_owner[3],
        by_owner[4],
        by_owner[5],
    )


def solution(mesh):
    rows = P(BOTH, None)
    return jax.shard_map(
        local,
        mesh=mesh,
        in_specs=(
            rows,
            P("dp", None),
            P(BOTH),
            P(BOTH),
            P("dp", "tensor"),
            P("tensor", None),
            P("dp", "tensor"),
            P("dp", "tensor"),
            P("tensor", None),
            P("tensor", "dp"),
            P(),
            P(),
            P(),
            P("dp", "tensor"),
            P("tensor", None),
            P("tensor", "dp"),
            P(),
            P(),
            P(),
            rows,
        ),
        out_specs=(
            rows,
            rows,
            P("dp", "tensor"),
            P("tensor", "dp"),
            P("dp", "tensor"),
            P("dp", "tensor"),
            P("tensor", "dp"),
            P("tensor", "dp"),
            P("dp"),
            P("dp"),
            P("dp"),
            P("dp", "tensor"),
            P("tensor", "dp"),
            P("tensor", "dp"),
            P("dp"),
            P("dp"),
            P("dp"),
        ),
        check_vma=False,
    )
```

```python
import functools

import jax
import jax.numpy as jnp
from jax import lax
from jax.experimental import pallas as pl
from jax.experimental.pallas import tpu as pltpu
from jax.sharding import PartitionSpec as P


EPSILON = 1e-12
INV_ROOT_TWO = 0.7071067811865476
INV_ROOT_TWO_PI = 0.3989422804014327
BF = jnp.bfloat16
F32 = jnp.float32
NN = (((1,), (0,)), ((), ()))
NT = (((1,), (1,)), ((), ()))
TN = (((0,), (0,)), ((), ()))
BOTH = ("dp", "tensor")
SPARE = 64
BIG = 67043328


def mm(left, right, dims):
    return lax.dot_general(left, right, dims, preferred_element_type=F32)


def swap(value, bit):
    ways = lax.axis_size("tensor")
    return lax.ppermute(value, "tensor", [(i, i ^ bit) for i in range(ways)])


def steps_of(groups, ways):
    far = [1 << i for i in range(groups.bit_length() - 1)]
    chips = [1 << i for i in range(ways.bit_length() - 1)]
    line = [("dp", bit) for bit in far[1:]]
    near = [("dp", bit) for bit in far[:1]]
    across = [("tensor", bit) for bit in chips[1:]]
    core = [("tensor", bit) for bit in chips[:1]]
    return (line + near + across + core, across + line + near + core)


def place_of(steps, g, t):
    place = 0
    for i, (axis, bit) in enumerate(steps):
        place += (((g if axis == "dp" else t) // bit) % 2) << i
    return place


def step_swap(value, step):
    axis, bit = step
    return lax.ppermute(value, axis, [(i, i ^ bit) for i in range(lax.axis_size(axis))])


def gather_steps(shard, steps):
    held = shard[None]
    for step in steps:
        held = jnp.concatenate((held, step_swap(held, step)), axis=0)
    return held


def sum_steps(blocks, steps):
    for step in steps[::-1]:
        half = blocks.shape[0] // 2
        arrived = step_swap(blocks[half:], step)
        blocks = (blocks[:half].astype(F32) + arrived.astype(F32)).astype(BF)
    return blocks[0].astype(F32)


def gather_group(value):
    across = swap(value, 2)
    return (value, swap(value, 1), across, swap(across, 1))


def vmem():
    return pltpu.CompilerParams(vmem_limit_bytes=BIG)


def whole_spec(array):
    return pl.BlockSpec(array.shape, lambda *_: (0,) * array.ndim)


def project_kernel(steps, me_ref, x_ref, *refs):
    b_ref, w_ref, q_ref, k_ref, v_ref = refs[-5:]
    width = x_ref.shape[1]
    if steps is None:
        g_ref = refs[0]
        ways = g_ref.shape[1]
        cols = width // ways
        for t in range(ways):
            for i, base in enumerate((2 * width, 0, width)):
                piece = g_ref[:, t, :, i * cols : (i + 1) * cols].reshape(width, cols)
                w_ref[:, base + t * cols : base + (t + 1) * cols] = piece
    else:
        groups, ways = steps[0]
        cols = width // ways
        part = width // groups
        half = part // 2
        for t in range(ways):
            for color in range(2):

                def fill(g, carry, t=t, color=color):
                    source = place_of(steps[1 + color], g, t)
                    block = refs[color].at[lax.bitwise_xor(source, me_ref[color])]
                    first = pl.multiple_of(g * part + color * half, 16)
                    for i, base in enumerate((2 * width, 0, width)):
                        w_ref[pl.ds(first, half), base + t * cols : base + (t + 1) * cols] = block[
                            :, i * cols : (i + 1) * cols
                        ]
                    return carry

                lax.fori_loop(0, groups, fill, 0)
    rows = x_ref[...]
    query = (mm(rows, w_ref[:, 2 * width :], NN) + b_ref[0:1, :]).astype(BF)
    q_ref[...] = (query.astype(F32) * 0.125).astype(BF)
    k_ref[...] = mm(rows, w_ref[:, :width], NN).astype(BF)
    v_ref[...] = (mm(rows, w_ref[:, width : 2 * width], NN) + b_ref[1:2, :]).astype(BF)


def project(x_own, gathered, bias, total, me_places, steps):
    rows, width = x_own.shape
    own = pl.BlockSpec((rows, width), lambda i, m: (0, 0))
    return pl.pallas_call(
        functools.partial(project_kernel, steps),
        grid_spec=pltpu.PrefetchScalarGridSpec(
            num_scalar_prefetch=1,
            grid=(1,),
            in_specs=[own] + [whole_spec(a) for a in gathered] + [whole_spec(bias)],
            out_specs=[pl.BlockSpec((width, 3 * width), lambda i, m: (0, 0)), own, own, own],
        ),
        out_shape=[
            jax.ShapeDtypeStruct((width, 3 * width), BF),
            jax.ShapeDtypeStruct((rows, width), BF),
            jax.ShapeDtypeStruct((total, width), BF),
            jax.ShapeDtypeStruct((total, width), BF),
        ],
        compiler_params=vmem(),
        cost_estimate=pl.CostEstimate(
            flops=6 * rows * width * width, bytes_accessed=16 * width * width, transcendentals=0
        ),
        name="project",
    )(me_places, x_own, *gathered, bias)


def project_more_kernel(x_ref, w_ref, b_ref, kin_ref, vin_ref, k_ref, v_ref):
    width = x_ref.shape[1]
    rows = x_ref[...]
    k_ref[...] = mm(rows, w_ref[:, :width], NN).astype(BF)
    v_ref[...] = (mm(rows, w_ref[:, width:], NN) + b_ref[1:2, :]).astype(BF)


def project_more(x_chunk, weights, bias, keys, values, chunk):
    rows, width = x_chunk.shape
    place = pl.BlockSpec((rows, width), lambda i: (chunk, 0))
    anywhere = pl.BlockSpec(memory_space=pl.ANY)
    return pl.pallas_call(
        project_more_kernel,
        grid=(1,),
        in_specs=[
            whole_spec(x_chunk),
            pl.BlockSpec((width, 2 * width), lambda i: (0, 0)),
            whole_spec(bias),
            anywhere,
            anywhere,
        ],
        out_specs=[place, place],
        out_shape=[jax.ShapeDtypeStruct(keys.shape, BF)] * 2,
        input_output_aliases={3: 0, 4: 1},
        compiler_params=vmem(),
        cost_estimate=pl.CostEstimate(
            flops=4 * rows * width * width, bytes_accessed=8 * width * width, transcendentals=0
        ),
        name="project_more",
    )(x_chunk, weights, bias, keys, values)


def attend_kernel(q_ref, k_ref, v_ref, segq_ref, segk_ref, ctx_ref, wide_ref, lse_ref):
    query = q_ref[...]
    keys = k_ref[...]
    values = v_ref[...]
    allowed = segq_ref[...] == segk_ref[...]
    half = lax.broadcasted_iota(jnp.int32, query.shape, 1) // 64
    mixed = jnp.zeros(query.shape, F32)
    stat = jnp.zeros(query.shape, F32)
    for head in range(2):
        mine = half == head
        scores = mm(jnp.where(mine, query, jnp.zeros_like(query)), keys, NT)
        scores = jnp.where(allowed, scores, -1e30)
        top = jnp.max(scores, axis=-1, keepdims=True)
        expo = jnp.exp(scores - top)
        total = jnp.sum(expo, axis=-1, keepdims=True)
        part = mm(expo.astype(BF), values, NN) / total
        mixed = jnp.where(mine, part, mixed)
        stat = jnp.where(mine, top + jnp.log(total), stat)
    ctx_ref[...] = mixed.astype(BF)
    wide_ref[...] = mixed
    turned = stat.T
    lse_ref[0, 0:1, :] = turned[0:1, :]
    lse_ref[0, 1:2, :] = turned[64:65, :]


def attend(query, keys, values, seg_col, seg_row):
    rows, width = query.shape
    total = keys.shape[0]
    block = min(256, rows)
    pairs = width // 128
    mine = pl.BlockSpec((block, 128), lambda p, i: (i, p))
    return pl.pallas_call(
        attend_kernel,
        grid=(pairs, rows // block),
        in_specs=[
            mine,
            pl.BlockSpec((total, 128), lambda p, i: (0, p)),
            pl.BlockSpec((total, 128), lambda p, i: (0, p)),
            pl.BlockSpec((block, 1), lambda p, i: (i, 0)),
            pl.BlockSpec((1, total), lambda p, i: (0, 0)),
        ],
        out_specs=[mine, mine, pl.BlockSpec((1, 2, block), lambda p, i: (p, 0, i))],
        out_shape=[
            jax.ShapeDtypeStruct((rows, width), BF),
            jax.ShapeDtypeStruct((rows, width), F32),
            jax.ShapeDtypeStruct((pairs, 2, rows), F32),
        ],
        compiler_params=vmem(),
        cost_estimate=pl.CostEstimate(
            flops=16 * rows * total * width,
            bytes_accessed=16 * rows * width,
            transcendentals=rows * total * width // 64,
        ),
        name="attend",
    )(query, keys, values, seg_col, seg_row)


def attend_back_kernel(last, *refs):
    q_ref, g_ref, k_ref, v_ref, lse_ref, inner_ref, segq_ref, segk_ref = refs[:8]
    before_ref = refs[8] if last else None
    dq_ref, dk_ref, dv_ref, acc = refs[-4:]
    chunk = pl.program_id(1)
    query = q_ref[...]
    grad = g_ref[...]
    keys = k_ref[...]
    values = v_ref[...]
    allowed = segk_ref[...] == segq_ref[...]
    half = lax.broadcasted_iota(jnp.int32, query.shape, 1) // 64
    half_k = lax.broadcasted_iota(jnp.int32, keys.shape, 1) // 64
    dk = jnp.zeros(keys.shape, F32)
    dv = jnp.zeros(keys.shape, F32)
    dq = jnp.zeros(acc.shape, F32)
    for head in range(2):
        mine = half == head
        q_head = jnp.where(mine, query, jnp.zeros_like(query))
        g_head = jnp.where(mine, grad, jnp.zeros_like(grad))
        k_head = jnp.where(half_k == head, keys, jnp.zeros_like(keys))
        scores = mm(keys, q_head, NT)
        probs = jnp.where(allowed, jnp.exp(scores - lse_ref[0, head : head + 1, :]), 0.0)
        grad_probs = mm(values, g_head, NT)
        grad_scores = (probs * (grad_probs - inner_ref[0, head : head + 1, :])).astype(BF)
        dv += mm(probs.astype(BF), g_head, NN)
        dk += mm(grad_scores, q_head, NN)
        dq += mm(k_head, grad_scores, TN)
    dk_ref[...] = dk.astype(BF)
    dv_ref[...] = dv.astype(BF)

    @pl.when(chunk == 0)
    def _():
        acc[...] = before_ref[...] + dq if last else dq

    @pl.when(chunk > 0)
    def _():
        acc[...] += dq

    @pl.when(chunk == pl.num_programs(1) - 1)
    def _():
        dq_ref[...] = (acc[...] * 0.125).T.astype(BF) if last else acc[...]


def attend_back(query, grad, keys, values, lse, inner, seg_row, seg_col, base, before):
    rows, width = query.shape
    last = before is not None
    own = pl.BlockSpec((rows, 128), lambda p, c: (0, p))
    far = pl.BlockSpec((rows, 128), lambda p, c: (base - c, p))
    out = pl.BlockSpec((rows, 128), lambda p, c: (c, p))
    stat = pl.BlockSpec((1, 2, rows), lambda p, c: (p, 0, 0))
    turned = pl.BlockSpec((128, rows), lambda p, c: (p, 0))
    if last:
        dq_spec, dq_shape = own, jax.ShapeDtypeStruct((rows, width), BF)
    else:
        dq_spec, dq_shape = turned, jax.ShapeDtypeStruct((width, rows), F32)
    return pl.pallas_call(
        functools.partial(attend_back_kernel, last),
        grid=(width // 128, 2),
        in_specs=[
            own,
            own,
            far,
            far,
            stat,
            stat,
            pl.BlockSpec((1, rows), lambda p, c: (0, 0)),
            pl.BlockSpec((rows, 1), lambda p, c: (base - c, 0)),
        ]
        + ([turned] if last else []),
        out_specs=[dq_spec, out, out],
        out_shape=[
            dq_shape,
            jax.ShapeDtypeStruct((2 * rows, width), BF),
            jax.ShapeDtypeStruct((2 * rows, width), BF),
        ],
        scratch_shapes=[pltpu.VMEM((128, rows), F32)],
        compiler_params=vmem(),
        cost_estimate=pl.CostEstimate(
            flops=80 * rows * rows * width,
            bytes_accessed=32 * rows * width,
            transcendentals=rows * rows * width // 32,
        ),
        name="attend_back",
    )(query, grad, keys, values, lse, inner, seg_row, seg_col, *([before] if last else []))


def tile_rows(vectors, count):
    row = lax.broadcasted_iota(jnp.int32, (count, SPARE), 0)
    tile = jnp.zeros((count, SPARE), F32)
    at = 0
    for vector in vectors:
        for first in range(0, vector.shape[1], SPARE):
            tile = jnp.where(row == at, vector[:, first : first + SPARE], tile)
            at += 1
    return tile


def middle_kernel(
    x_ref, ctx_ref, wide_ref, cot_ref, vec_ref, bu_ref, wu_ref, wd_ref, tail_ref,
    y_ref, dh1_ref, dctx_ref, inner_ref, small_ref, grads_ref,
    wo, xhat, scale, n1b, acc, act, slope, df, gmain, gtail, sems,
):
    step = pl.program_id(0)
    ways = tail_ref.shape[1]
    outer, inner_rows = tail_ref.shape[0], tail_ref.shape[2]
    _, width = x_ref.shape
    cols = width // ways

    def vec(i):
        return vec_ref[i : i + 1, :]

    @pl.when(step == 0)
    def _():
        for t in range(ways):
            wo[:, t * cols : (t + 1) * cols] = tail_ref[:, t, :, :cols].reshape(width, cols)
        h1 = x_ref[...].astype(F32) + mm(ctx_ref[...], wo[...], NT) + vec(0)
        n1, normal, size = norm_forward(h1, vec(1), vec(2))
        xhat[...] = normal
        scale[...] = size
        n1b[...] = n1.astype(BF)
        acc[...] = n1 + vec(3)

    @pl.when(step < ways)
    def _():
        pre = mm(n1b[...], wu_ref[...].reshape(width, width), NN) + bu_ref[0]
        value, rate = gelu_parts(pre)
        value = value.astype(BF)
        act[step] = value
        slope[step] = rate
        acc[...] += mm(value, wd_ref[...].reshape(width, width), NT)

    @pl.when(step == ways - 1)
    def _():
        y, normal, size = norm_forward(acc[...], vec(4), vec(5))
        y_ref[...] = y.astype(BF)
        grad = cot_ref[...].astype(F32)
        small_ref[4:5, :] = jnp.sum(grad * normal, axis=0, keepdims=True)
        small_ref[5:6, :] = jnp.sum(grad, axis=0, keepdims=True)
        dh2 = norm_backward(grad, normal, size, vec(4))
        low = dh2.astype(BF)
        df[...] = low
        small_ref[3:4, :] = jnp.sum(low.astype(F32), axis=0, keepdims=True)
        acc[...] = dh2

    def main_copy(t):
        return pltpu.make_async_copy(
            gmain.at[t], grads_ref.at[:, t, :, pl.ds(0, 2 * width)], sems.at[t]
        )

    def tail_copy(t):
        return pltpu.make_async_copy(
            gtail.at[t], grads_ref.at[:, t, :, pl.ds(2 * width, cols + SPARE)], sems.at[ways + t]
        )

    @pl.when(step >= ways)
    def _():
        t = step - ways
        du = (mm(df[...], wd_ref[...].reshape(width, width), NN) * slope[t]).astype(BF)
        small_ref[pl.ds(8 + t, 1), :] = jnp.sum(du.astype(F32), axis=0, keepdims=True)
        shape = (outer, inner_rows, width)
        gmain[t, :, :, :width] = mm(n1b[...], du, TN).astype(BF).reshape(shape)
        gmain[t, :, :, width:] = mm(df[...], act[t], TN).astype(BF).reshape(shape)
        main_copy(t).start()
        acc[...] += mm(du, wu_ref[...].reshape(width, width), NT)

    @pl.when(step == 2 * ways - 1)
    def _():
        dn1 = acc[...]
        normal = xhat[...]
        small_ref[1:2, :] = jnp.sum(dn1 * normal, axis=0, keepdims=True)
        small_ref[2:3, :] = jnp.sum(dn1, axis=0, keepdims=True)
        dh1 = norm_backward(dn1, normal, scale[...], vec(1))
        low = dh1.astype(BF)
        dh1_ref[...] = dh1
        small_ref[0:1, :] = jnp.sum(low.astype(F32), axis=0, keepdims=True)
        g_wo = mm(low, ctx_ref[...], TN).astype(BF)
        spare = jnp.zeros((width // outer, SPARE), F32)
        vectors = [small_ref[i : i + 1, :] for i in range(6)]
        for t in range(ways):
            gtail[t, :, :, :cols] = g_wo[:, t * cols : (t + 1) * cols].reshape(
                outer, inner_rows, cols
            )
            if outer > 1:
                spare = tile_rows([small_ref[8 + t : 9 + t, :]] + vectors, inner_rows)
                for g in range(outer):
                    gtail[t, g, :, cols:] = spare.astype(BF)
            else:
                gtail[t, :, :, cols:] = jnp.zeros((outer, inner_rows, SPARE), BF)
            tail_copy(t).start()
        dctx = mm(low, wo[...], NN).astype(BF)
        dctx_ref[...] = dctx
        head = lax.broadcasted_iota(jnp.int32, (16, width), 0)
        lane = lax.broadcasted_iota(jnp.int32, (16, width), 1) // 64
        inner_ref[...] = lax.dot_general(
            (head == lane).astype(F32),
            dctx.astype(F32) * wide_ref[...],
            NT,
            preferred_element_type=F32,
            precision=lax.Precision.HIGHEST,
        )
        for t in range(ways):
            main_copy(t).wait()
            tail_copy(t).wait()


def middle(x_own, context, wide, cot, vectors, bu, gathered):
    rows, width = x_own.shape
    outer, ways, inner_rows, _ = gathered.shape
    cols = width // ways
    half = (outer, 1, inner_rows, width)
    return pl.pallas_call(
        middle_kernel,
        grid=(2 * ways,),
        in_specs=[
            whole_spec(x_own),
            whole_spec(context),
            whole_spec(wide),
            whole_spec(cot),
            whole_spec(vectors),
            pl.BlockSpec((1, 1, width), lambda s: (lax.rem(s, ways), 0, 0)),
            pl.BlockSpec(half, lambda s: (0, lax.rem(s, ways), 0, 0)),
            pl.BlockSpec(half, lambda s: (0, lax.rem(s, ways), 0, 1)),
            pl.BlockSpec(
                (outer, ways, inner_rows, cols + SPARE),
                lambda s: (0, 0, 0, 2 * width // (cols + SPARE)),
            ),
        ],
        out_specs=[
            whole_spec(x_own),
            whole_spec(x_own),
            whole_spec(x_own),
            pl.BlockSpec((16, rows), lambda s: (0, 0)),
            pl.BlockSpec((16, width), lambda s: (0, 0)),
            pl.BlockSpec(memory_space=pl.ANY),
        ],
        out_shape=[
            jax.ShapeDtypeStruct((rows, width), BF),
            jax.ShapeDtypeStruct((rows, width), F32),
            jax.ShapeDtypeStruct((rows, width), BF),
            jax.ShapeDtypeStruct((16, rows), F32),
            jax.ShapeDtypeStruct((16, width), F32),
            jax.ShapeDtypeStruct(gathered.shape, BF),
        ],
        scratch_shapes=[
            pltpu.VMEM((width, width), BF),
            pltpu.VMEM((rows, width), F32),
            pltpu.VMEM((rows, 1), F32),
            pltpu.VMEM((rows, width), BF),
            pltpu.VMEM((rows, width), F32),
            pltpu.VMEM((ways, rows, width), BF),
            pltpu.VMEM((ways, rows, width), F32),
            pltpu.VMEM((rows, width), BF),
            pltpu.VMEM((ways, outer, inner_rows, 2 * width), BF),
            pltpu.VMEM((ways, outer, inner_rows, cols + SPARE), BF),
            pltpu.SemaphoreType.DMA((2 * ways,)),
        ],
        compiler_params=vmem(),
        cost_estimate=pl.CostEstimate(
            flops=54 * rows * width * width,
            bytes_accessed=64 * width * width,
            transcendentals=8 * rows * width,
        ),
        name="middle",
    )(x_own, context, wide, cot, vectors, bu, gathered, gathered, gathered)


def terms_kernel(last, *refs):
    dk_ref, dv_ref, w_ref = refs[:3]
    first_ref, second_ref = refs[-2:]
    rows, width = first_ref.shape
    for i, out_ref in enumerate((first_ref, second_ref)):
        value = mm(dk_ref[i * rows : (i + 1) * rows, :], w_ref[:, :width], NT)
        value += mm(dv_ref[i * rows : (i + 1) * rows, :], w_ref[:, width : 2 * width], NT)
        if last and i == 1:
            value += mm(refs[3][...], w_ref[:, 2 * width :], NT) + refs[4][...]
        out_ref[...] = value.astype(out_ref.dtype)


def terms(dk, dv, weights, dq=None, dh1=None):
    rows, width = dk.shape[0] // 2, dk.shape[1]
    last = dq is not None
    args = (dk, dv, weights) + ((dq, dh1) if last else ())
    out = pl.BlockSpec((rows, width), lambda i: (0, 0))
    in_specs = [whole_spec(a) for a in args]
    if not last:
        in_specs[2] = pl.BlockSpec((width, 2 * width), lambda i: (0, 0))
    return pl.pallas_call(
        functools.partial(terms_kernel, last),
        grid=(1,),
        in_specs=in_specs,
        out_specs=[out, out],
        out_shape=[
            jax.ShapeDtypeStruct((rows, width), BF),
            jax.ShapeDtypeStruct((rows, width), F32),
        ],
        compiler_params=vmem(),
        cost_estimate=pl.CostEstimate(
            flops=8 * rows * width * width, bytes_accessed=8 * width * width, transcendentals=0
        ),
        name="terms",
    )(*args)


def weight_grads_kernel(steps, me_ref, x0, x1, x2, x3, dka, dva, dkb, dvb, dq_ref, *outs):
    small_ref = outs[-1]
    rows, width = x0.shape
    if steps is None:
        groups, ways = 1, outs[0].shape[1]
    else:
        groups, ways = steps[0]
    cols = width // ways
    part = width // groups
    half = part // 2

    def put(t, lanes, value):
        if steps is None:
            outs[0][0, t, :, lanes] = value
            return
        for g in range(groups):
            for color in range(2):
                place = lax.bitwise_xor(place_of(steps[1 + color], g, t), me_ref[color])
                first = g * part + color * half
                outs[color][place, :, lanes] = value[first : first + half, :]

    def keep(grad, i):
        low = grad.astype(BF)
        for t in range(ways):
            put(t, slice(i * cols, (i + 1) * cols), low[:, t * cols : (t + 1) * cols])

    def over_chunks(high, low):
        return (
            mm(x3[...], high[:rows, :], TN)
            + mm(x2[...], high[rows:, :], TN)
            + mm(x1[...], low[:rows, :], TN)
            + mm(x0[...], low[rows:, :], TN)
        )

    keep(mm(x0[...], dq_ref[...], TN), 0)
    keep(over_chunks(dka, dkb), 1)
    keep(over_chunks(dva, dvb), 2)
    g_bq = jnp.sum(dq_ref[...].astype(F32), axis=0, keepdims=True)
    g_bv = jnp.sum(dva[...].astype(F32), axis=0, keepdims=True)
    g_bv += jnp.sum(dvb[...].astype(F32), axis=0, keepdims=True)
    small_ref[0:1, :] = g_bq
    small_ref[1:2, :] = g_bv
    for t in range(ways):
        spare = slice(3 * cols, 3 * cols + SPARE)
        if steps is None:
            put(t, spare, jnp.zeros((width, SPARE), BF))
        else:
            here = slice(t * cols, (t + 1) * cols)
            tile = tile_rows([g_bq[:, here], g_bv[:, here]], half).astype(BF)
            put(t, spare, jnp.concatenate([tile] * (2 * groups), axis=0))


def weight_grads(chunks, dka, dva, dkb, dvb, dq, me_places, steps, ways):
    rows, width = dq.shape
    args = (*chunks, dka, dva, dkb, dvb, dq)
    lanes = 3 * width // ways + SPARE
    if steps is None:
        shapes = [(1, ways, width, lanes)]
    else:
        groups = steps[0][0]
        shapes = [(groups * ways, width // groups // 2, lanes)] * 2
    return pl.pallas_call(
        functools.partial(weight_grads_kernel, steps),
        grid_spec=pltpu.PrefetchScalarGridSpec(
            num_scalar_prefetch=1,
            grid=(1,),
            in_specs=[whole_spec(a) for a in args],
            out_specs=[
                pl.BlockSpec(s, lambda i, m, n=len(s): (0,) * n) for s in shapes + [(8, width)]
            ],
        ),
        out_shape=[jax.ShapeDtypeStruct(s, BF) for s in shapes]
        + [jax.ShapeDtypeStruct((8, width), F32)],
        compiler_params=vmem(),
        cost_estimate=pl.CostEstimate(
            flops=18 * rows * width * width, bytes_accessed=16 * width * width, transcendentals=0
        ),
        name="weight_grads",
    )(me_places, *args)


def norm_forward(value, gain, bias):
    centre = value - jnp.mean(value, axis=-1, keepdims=True)
    spread_sq = jnp.mean(centre * centre, axis=-1, keepdims=True)
    scale = lax.rsqrt(spread_sq + EPSILON)
    normal = centre * scale
    return (normal * gain + bias, normal, scale)


def norm_backward(grad, normal, scale, gain):
    scaled = grad * gain
    return scale * (
        scaled
        - jnp.mean(scaled, axis=-1, keepdims=True)
        - normal * jnp.mean(scaled * normal, axis=-1, keepdims=True)
    )


def gelu_parts(value):
    cdf = 0.5 * (1.0 + jax.scipy.special.erf(value * INV_ROOT_TWO))
    return value * cdf, cdf + value * jnp.exp(-0.5 * value * value) * INV_ROOT_TWO_PI


def layer(
    tokens,
    lengths,
    perm,
    inv,
    w_query,
    b_query,
    w_key,
    w_value,
    b_value,
    w_out,
    b_out,
    gain_one,
    bias_one,
    w_up,
    b_up,
    w_down,
    b_down,
    gain_two,
    bias_two,
    cotangent,
):
    rows, width = tokens.shape
    groups = lax.axis_size("dp")
    ways = lax.axis_size("tensor")
    me_dp = lax.axis_index("dp")
    me = lax.axis_index("tensor")
    per_peer = rows // groups
    part = width // groups
    cols = w_query.shape[1]
    slots = lengths.shape[1]
    heads_here = b_query.shape[0]
    aligned = part % 16 == 0 and part >= 96
    iota = jnp.arange(rows, dtype=jnp.int32)

    def for_kernel(gathered):
        grid = gathered.reshape(groups, ways, part, -1)
        if aligned:
            return grid
        return grid.transpose(1, 0, 2, 3).reshape(1, ways, width, -1)

    def for_owners(grads):
        if not aligned:
            grads = grads.reshape(ways, groups, part, -1).transpose(1, 0, 2, 3)
        return grads.reshape(groups * ways * part, -1)

    def gather_shards(shard):
        return for_kernel(lax.all_gather(shard, BOTH, axis=0, tiled=True))

    def sum_shards(grads):
        return lax.psum_scatter(
            for_owners(grads), BOTH, scatter_dimension=0, tiled=True
        ).astype(F32)

    spare = jnp.zeros((part, SPARE), BF)
    qkv_shard = jnp.concatenate((w_query, w_key, w_value, spare), axis=1)
    ffn_shard = jnp.concatenate((w_up, w_down.T, w_out.T, spare), axis=1)
    if aligned:
        orders = steps_of(groups, ways)
        steps = ((groups, ways),) + orders
        me_places = jnp.stack([place_of(order, me_dp, me) for order in orders]).astype(jnp.int32)
        middle_row = part // 2
        qkv_all = [
            gather_steps(qkv_shard[:middle_row], orders[0]),
            gather_steps(qkv_shard[middle_row:], orders[1]),
        ]
    else:
        steps = None
        me_places = jnp.zeros((2,), jnp.int32)
        qkv_all = [gather_shards(qkv_shard)]
    ffn_all = gather_shards(ffn_shard)

    slot = jnp.sum((inv[None, :] < inv[:, None]).astype(jnp.int32), axis=1)
    pick = (iota[:, None] == slot[None, :]).astype(BF)

    def to_dealt(value):
        packed = mm(pick, value, NN).astype(BF).reshape(groups, per_peer, width)
        return lax.all_to_all(packed, "dp", split_axis=0, concat_axis=0, tiled=True).reshape(
            rows, width
        )

    def to_given(value):
        packed = value.reshape(groups, per_peer, width)
        moved = lax.all_to_all(packed, "dp", split_axis=0, concat_axis=0, tiled=True)
        return mm(pick, moved.reshape(rows, width), TN).astype(BF)

    x_own = to_dealt(tokens)
    cot = to_dealt(cotangent)

    source = perm // rows // ways
    earlier = (source[None, :] == source[:, None]) & (iota[None, :] < iota[:, None])
    arrival = source * per_peer + jnp.sum(earlier.astype(jnp.int32), axis=1)
    cumulative = jnp.cumsum(lengths[0])
    places = me * rows + iota
    segment = jnp.sum((cumulative[None, :] <= places[:, None]).astype(jnp.int32), axis=1)
    seg_own = jnp.sum(
        jnp.where(iota[:, None] == arrival[None, :], segment[None, :], 0), axis=1
    ).astype(BF)
    message = jnp.concatenate(
        (seg_own, b_query.reshape(-1), b_value.reshape(-1), b_up.reshape(-1))
    )
    message = jnp.stack(gather_group(message.reshape(-1, 128))).reshape(ways, -1)
    seg_all = message[:, :rows].reshape(-1).astype(jnp.int32)
    seg_all = jnp.where(
        seg_all < slots, seg_all, slots + jnp.arange(ways * rows, dtype=jnp.int32)
    )
    biases = message[:, rows:][me ^ jnp.arange(ways)].astype(F32)
    qv_bias = jnp.stack(
        (biases[:, :cols].reshape(-1), biases[:, cols : 2 * cols].reshape(-1))
    )
    up_bias = biases[:, 2 * cols :].reshape(ways, 1, -1)
    vectors = jnp.stack(
        (b_out, gain_one, bias_one, b_down, gain_two, bias_two, b_out, b_out)
    ).astype(F32)

    chunks = gather_group(x_own)
    weights, query, keys, values = project(
        x_own, qkv_all, qv_bias, ways * rows, me_places, steps
    )
    for i in range(1, ways):
        keys, values = project_more(chunks[i], weights, qv_bias, keys, values, i)
    context, wide, lse = attend(
        query, keys, values, seg_all[:rows].reshape(rows, 1), seg_all.reshape(1, -1)
    )
    y, dh1, dctx, inner, small_ffn, ffn_grads = middle(
        x_own, context, wide, cot, vectors, up_bias, ffn_all
    )
    output = to_given(y)
    ffn_sum = sum_shards(ffn_grads)

    inner = inner[: width // 64].reshape(lse.shape)
    seg_row = seg_all[:rows].reshape(1, rows)
    seg_col = seg_all.reshape(-1, 1)
    dq_part, dka, dva = attend_back(
        query, dctx, keys, values, lse, inner, seg_row, seg_col, 3, None
    )
    term_3, term_2 = terms(dka, dva, weights)
    far = (term_2 + swap(term_3, 1).astype(F32)).astype(BF)
    dq_part, far = lax.optimization_barrier((dq_part, far))
    across = swap(far, 2)
    dq, dkb, dvb = attend_back(query, dctx, keys, values, lse, inner, seg_row, seg_col, 1, dq_part)
    *qkv_grads, small_qkv = weight_grads(
        chunks, dka, dva, dkb, dvb, dq, me_places, steps, ways
    )
    term_1, mine = terms(dkb, dvb, weights, dq, dh1)
    near = swap(term_1, 1)
    input_grad = to_given((mine + near.astype(F32) + across.astype(F32)).astype(BF))
    if aligned:
        sums = [sum_steps(grads, order) for grads, order in zip(qkv_grads, orders)]
        qkv_sum = jnp.concatenate(sums, axis=0)
    else:
        qkv_sum = sum_shards(qkv_grads[0])

    def my_lanes(vector):
        lanes = vector.reshape(heads_here, groups, -1)
        return lax.dynamic_index_in_dim(lanes, me_dp, 1, keepdims=False)

    if aligned:
        from_ffn = ffn_sum[:, 2 * width + cols :].reshape(-1)
        g_bup = from_ffn[:width]
        by_width = from_ffn[width : 7 * width].reshape(6, width)
        from_qkv = qkv_sum[:, 3 * cols :].reshape(-1)
        g_bq, g_bv = from_qkv[:cols], from_qkv[cols : 2 * cols]
    else:
        small = lax.psum(jnp.concatenate((small_ffn, small_qkv)).astype(BF), BOTH).astype(F32)
        by_width = small[:6]
        g_bup = lax.dynamic_index_in_dim(small, 8 + me, 0, keepdims=False)
        g_bq = lax.dynamic_slice_in_dim(small[16], me * cols, cols)
        g_bv = lax.dynamic_slice_in_dim(small[17], me * cols, cols)
    by_owner = lax.dynamic_slice_in_dim(by_width, me_dp * part, part, 1)
    return (
        output,
        input_grad,
        qkv_sum[:, :cols],
        my_lanes(g_bq),
        qkv_sum[:, cols : 2 * cols],
        qkv_sum[:, 2 * cols : 3 * cols],
        my_lanes(g_bv),
        ffn_sum[:, 2 * width : 2 * width + cols].T,
        by_owner[0],
        by_owner[1],
        by_owner[2],
        ffn_sum[:, :width],
        my_lanes(g_bup),
        ffn_sum[:, width : 2 * width].T,
        by_owner[3],
        by_owner[4],
        by_owner[5],
    )


def solution(mesh):
    rows = P(BOTH, None)
    return jax.shard_map(
        layer,
        mesh=mesh,
        in_specs=(
            rows,
            P("dp", None),
            P(BOTH),
            P(BOTH),
            P("dp", "tensor"),
            P("tensor", None),
            P("dp", "tensor"),
            P("dp", "tensor"),
            P("tensor", None),
            P("tensor", "dp"),
            P(),
            P(),
            P(),
            P("dp", "tensor"),
            P("tensor", None),
            P("tensor", "dp"),
            P(),
            P(),
            P(),
            rows,
        ),
        out_specs=(
            rows,
            rows,
            P("dp", "tensor"),
            P("tensor", "dp"),
            P("dp", "tensor"),
            P("dp", "tensor"),
            P("tensor", "dp"),
            P("tensor", "dp"),
            P("dp"),
            P("dp"),
            P("dp"),
            P("dp", "tensor"),
            P("tensor", "dp"),
            P("tensor", "dp"),
            P("dp"),
            P("dp"),
            P("dp"),
        ),
        check_vma=False,
    )
```
